32 devices in a mesh: clip: 8 (over z, x), row: 4 (over y, core).
Axes of the slice: x: 2, y: 2, z: 4, core: 2. Of those that a mesh axis runs over, the one named last changes fastest.
Arguments:
- features: bfloat16 [8, 128, 32, 256], P('clip', None, 'row'), may hold values from -6 to 6
- out_weight: bfloat16 [3, 128, 3, 3], replicated, may hold values from -0.1875 to 0.1875
- out_bias: float32 [3], replicated, may hold values from -0.5 to 0.5
- targets: bfloat16 [8, 3, 32, 256], P('clip', None, 'row'), may hold values from -1 to 1
- weight_one: bfloat16 [64, 3, 3, 3], replicated, may hold values from -1.25 to 1.25
- bias_one: float32 [64], replicated, may hold values from -0.2 to 0.2
- weight_two: bfloat16 [64, 64, 3, 3], replicated, may hold values from -0.375 to 0.375
- bias_two: float32 [64], replicated, may hold values from -0.2 to 0.2
- weight_three: bfloat16 [128, 64, 3, 3], replicated, may hold values from -0.375 to 0.375
- bias_three: float32 [128], replicated, may hold values from -0.2 to 0.2
- weight_four: bfloat16 [128, 128, 3, 3], replicated, may hold values from -0.25 to 0.25
- bias_four: float32 [128], replicated, may hold values from -0.2 to 0.2
- lin_one: float32 [64], replicated, may hold values from 0.05 to 0.5
- lin_two: float32 [128], replicated, may hold values from 0.05 to 0.5
Outputs:
- loss: float32 [], replicated
- feature_grad: bfloat16 [8, 128, 32, 256], P('clip', None, 'row')
- out_weight_grad: float32 [3, 128, 3, 3], replicated
- out_bias_grad: float32 [3], replicated
The draws below stay inside these ranges and needn't reach their ends.
All inputs are finite; a program needn't handle non-finite values.
Results may differ from the reference program's by a relative error of at most 0.02.
Values may be sent and summed in bfloat16 or wider, within the bound.
A program may use at most 64 MiB of HBM per device.

```python
import math
import jax
import jax.numpy as jnp
from jax import lax

CF = 128
C1 = 64
C2 = 128
W = 256
H = 32
FRAMES = 8


def shard_levels(own_key, extent, split, least, top_value):
    def one(dim, blocks):
        steps = jax.random.uniform(jax.random.fold_in(jax.random.fold_in(own_key, 6), dim), (blocks,), jnp.float32, least / len(split), top_value / len(split))
        return jnp.repeat(jnp.exp(steps), extent[dim] // blocks).reshape((-1,) + (1,) * (len(extent) - dim - 1))

    gain = one(*split[0])
    for cut in split[1:]:
        gain = gain * one(*cut)
    return gain


def gaussian(rng, dims, scale, limit, shards=(), kind=jnp.bfloat16):
    entries = scale * jax.random.normal(rng, dims, jnp.float32)
    if shards:
        entries = entries * shard_levels(rng, dims, shards, -0.22, 0.18)
    return jnp.clip(entries, -limit, limit).astype(kind)


def setup_inputs(seed: int = 0) -> dict:
    streams_of = jax.random.split(jax.random.key(seed), 15)
    features = gaussian(streams_of[0], (FRAMES, CF, H, W), 1.0, 6.0, ((0, 8), (2, 4)))
    out_weight = gaussian(streams_of[1], (3, CF, 3, 3), (9 * CF) ** -0.5, 0.1875)
    out_bias = jnp.clip(jax.random.uniform(streams_of[2], (3,), jnp.float32, -0.5, 0.5), -0.5, 0.5)
    targets = jnp.clip(jax.random.uniform(streams_of[3], (FRAMES, 3, H, W), jnp.float32, -1.0, 1.0) * shard_levels(streams_of[3], (FRAMES, 3, H, W), ((0, 8), (2, 4)), -0.4, 0.0), -1.0, 1.0).astype(jnp.bfloat16)
    weight_one = gaussian(streams_of[4], (C1, 3, 3, 3), 27 ** -0.5, 1.25)
    bias_one = jnp.clip(jax.random.uniform(streams_of[5], (C1,), jnp.float32, -0.2, 0.2), -0.2, 0.2)
    weight_two = gaussian(streams_of[6], (C1, C1, 3, 3), (9 * C1 // 2) ** -0.5, 0.375)
    bias_two = jnp.clip(jax.random.uniform(streams_of[7], (C1,), jnp.float32, -0.2, 0.2), -0.2, 0.2)
    weight_three = gaussian(streams_of[8], (C2, C1, 3, 3), (9 * C1 // 2) ** -0.5, 0.375)
    bias_three = jnp.clip(jax.random.uniform(streams_of[9], (C2,), jnp.float32, -0.2, 0.2), -0.2, 0.2)
    weight_four = gaussian(streams_of[10], (C2, C2, 3, 3), (9 * C2 // 2) ** -0.5, 0.25)
    bias_four = jnp.clip(jax.random.uniform(streams_of[11], (C2,), jnp.float32, -0.2, 0.2), -0.2, 0.2)
    lin_one = jnp.clip(jnp.exp(jax.random.uniform(streams_of[12], (C1,), jnp.float32, math.log(0.05), math.log(0.5))), 0.05, 0.5)
    lin_two = jnp.clip(jnp.exp(jax.random.uniform(streams_of[13], (C2,), jnp.float32, math.log(0.05), math.log(0.5))), 0.05, 0.5)
    return {"features": features, "out_weight": out_weight, "out_bias": out_bias, "targets": targets, "weight_one": weight_one, "bias_one": bias_one, "weight_two": weight_two, "bias_two": bias_two, "weight_three": weight_three, "bias_three": bias_three, "weight_four": weight_four, "bias_four": bias_four, "lin_one": lin_one, "lin_two": lin_two}


shift_values = [-0.03, -0.088, -0.188]
scale_values = [0.458, 0.448, 0.45]

def shift_array():
    return jnp.array(shift_values, jnp.float32).reshape(1, 3, 1, 1)

def scale_array():
    return jnp.array(scale_values, jnp.float32).reshape(1, 3, 1, 1)

def gelu_exact(values):
    return values * 0.5 * (1.0 + jax.scipy.special.erf(values / math.sqrt(2.0)))

def gelu_slope(values):
    normal_cdf = 0.5 * (1.0 + jax.scipy.special.erf(values / math.sqrt(2.0)))
    density = jnp.exp(-0.5 * values * values) / math.sqrt(2.0 * math.pi)
    return normal_cdf + values * density

def pad_rows(inputs):
    return jnp.pad(inputs, ((0, 0), (0, 0), (1, 1), (0, 0)))

def flipped(weight):
    return jnp.flip(weight, (2, 3)).transpose(1, 0, 2, 3)

def conv_valid(padded, weight):
    frame_count, channels, row_total, col_count = padded.shape
    row_count = row_total - 2
    outputs = weight.shape[0]
    wide = jnp.pad(padded, ((0, 0), (0, 0), (0, 0), (1, 1)))
    results = []
    for frame_pos in range(frame_count):
        total = jnp.zeros((outputs, row_count * col_count), jnp.float32)
        for row_shift in range(3):
            for col_shift in range(3):
                piece = wide[frame_pos, :, row_shift:row_shift + row_count, col_shift:col_shift + col_count]
                total = total + jnp.dot(weight[:, :, row_shift, col_shift], piece.reshape(channels, row_count * col_count), preferred_element_type=jnp.float32)
        results.append(total.reshape(outputs, row_count, col_count))
    return jnp.stack(results)

def grad_from_input(grad_out, padded):
    frame_count, channels, row_total, col_count = padded.shape
    row_count = row_total - 2
    outputs = grad_out.shape[1]
    wide = jnp.pad(padded, ((0, 0), (0, 0), (0, 0), (1, 1)))
    blocks = []
    for row_shift in range(3):
        for col_shift in range(3):
            total = jnp.zeros((outputs, channels), jnp.float32)
            for frame_pos in range(frame_count):
                piece = wide[frame_pos, :, row_shift:row_shift + row_count, col_shift:col_shift + col_count].reshape(channels, row_count * col_count)
                left = grad_out[frame_pos].reshape(outputs, row_count * col_count)
                total = total + lax.dot_general(left, piece, (((1,), (1,)), ((), ())), preferred_element_type=jnp.float32)
            blocks.append(total)
    return jnp.stack(blocks).reshape(3, 3, outputs, channels).transpose(2, 3, 0, 1)

def pool_mean(values):
    frame_count, channels, row_count, col_count = values.shape
    return values.reshape(frame_count, channels, row_count // 2, 2, col_count // 2, 2).mean(axis=(3, 5))

def upsample(values):
    return jnp.repeat(jnp.repeat(values, 2, 2), 2, 3)

def vgg_forward(image, weights):
    weight_one, bias_one, weight_two, bias_two, weight_three, bias_three, weight_four, bias_four = weights
    pre_one = conv_valid(pad_rows(image), weight_one) + bias_one[None, :, None, None]
    act_one = gelu_exact(pre_one).astype(jnp.bfloat16)
    pre_two = conv_valid(pad_rows(act_one), weight_two) + bias_two[None, :, None, None]
    act_two = gelu_exact(pre_two)
    pooled = pool_mean(act_two).astype(jnp.bfloat16)
    pre_three = conv_valid(pad_rows(pooled), weight_three) + bias_three[None, :, None, None]
    act_three = gelu_exact(pre_three).astype(jnp.bfloat16)
    pre_four = conv_valid(pad_rows(act_three), weight_four) + bias_four[None, :, None, None]
    act_four = gelu_exact(pre_four)
    return (pre_one, pre_two, act_two, pre_three, pre_four, act_four)

def lpips_layer(feat_dec, feat_tgt, lin, count):
    norm_dec = jnp.sqrt(lax.optimization_barrier(jnp.sum(feat_dec * feat_dec, 1, keepdims=True)) + 1e-06)
    norm_tgt = jnp.sqrt(lax.optimization_barrier(jnp.sum(feat_tgt * feat_tgt, 1, keepdims=True)) + 1e-06)
    unit_dec = feat_dec / norm_dec
    differ = unit_dec - feat_tgt / norm_tgt
    scaled = lin[None, :, None, None]
    part = jnp.sum(scaled * differ * differ) / count
    grad_unit = 2.0 * scaled * differ / count
    grad_feat = (grad_unit - unit_dec * lax.optimization_barrier(jnp.sum(grad_unit * unit_dec, 1, keepdims=True))) / norm_dec
    return (part, grad_feat)

def one_frame(pair, out_weight, out_bias, weights, lin_one, lin_two):
    features = pair[0][None]
    targets = pair[1][None]
    weight_one, bias_one, weight_two, bias_two, weight_three, bias_three, weight_four, bias_four = weights
    height = features.shape[2]
    width = features.shape[3]
    feat_pad = pad_rows(features)
    decoded = (conv_valid(feat_pad, out_weight) + out_bias[None, :, None, None]).astype(jnp.bfloat16)
    image_dec = ((decoded.astype(jnp.float32) - shift_array()) / scale_array()).astype(jnp.bfloat16)
    image_tgt = ((targets.astype(jnp.float32) - shift_array()) / scale_array()).astype(jnp.bfloat16)
    pre_one, pre_two, act_two, pre_three, pre_four, act_four = vgg_forward(image_dec, weights)
    tgt_acts = vgg_forward(image_tgt, weights)
    part_one, grad_two = lpips_layer(act_two, tgt_acts[2], lin_one, float(height * width))
    part_two, grad_four = lpips_layer(act_four, tgt_acts[5], lin_two, float(height // 2 * (width // 2)))
    grad_pre4 = (grad_four * gelu_slope(pre_four)).astype(jnp.bfloat16)
    grad_act3 = conv_valid(pad_rows(grad_pre4), flipped(weight_four))
    grad_pre3 = (grad_act3 * gelu_slope(pre_three)).astype(jnp.bfloat16)
    grad_pool = conv_valid(pad_rows(grad_pre3), flipped(weight_three))
    grad_pre2 = ((grad_two + 0.25 * upsample(grad_pool)) * gelu_slope(pre_two)).astype(jnp.bfloat16)
    grad_act1 = conv_valid(pad_rows(grad_pre2), flipped(weight_two))
    grad_pre1 = (grad_act1 * gelu_slope(pre_one)).astype(jnp.bfloat16)
    grad_image = conv_valid(pad_rows(grad_pre1), flipped(weight_one))
    grad_dec = (grad_image / scale_array()).astype(jnp.bfloat16)
    feature_grad = conv_valid(pad_rows(grad_dec), flipped(out_weight)).astype(jnp.bfloat16)
    weight_grad = grad_from_input(grad_dec, feat_pad)
    bias_grad = lax.optimization_barrier(jnp.sum(grad_dec.astype(jnp.float32), (0, 2, 3)))
    return (part_one + part_two, feature_grad[0], weight_grad, bias_grad)

def reference(features, out_weight, out_bias, targets, weight_one, bias_one, weight_two, bias_two, weight_three, bias_three, weight_four, bias_four, lin_one, lin_two):
    weights = (weight_one, bias_one, weight_two, bias_two, weight_three, bias_three, weight_four, bias_four)

    def runner(pair):
        return one_frame(pair, out_weight, out_bias, weights, lin_one, lin_two)
    parts, feature_grad, weight_grads, bias_grads = lax.map(runner, (features, targets))
    return (jnp.sum(parts), feature_grad, lax.optimization_barrier(jnp.sum(weight_grads, 0)), lax.optimization_barrier(jnp.sum(bias_grads, 0)))
```

```python
import functools
import math

import jax
import jax.numpy as jnp
from jax import lax
from jax.experimental import pallas as pl
from jax.experimental.pallas import tpu as pltpu
from jax.sharding import PartitionSpec as P

shift_values = [-0.03, -0.088, -0.188]
scale_values = [0.458, 0.448, 0.45]

F32, BF16 = jnp.float32, jnp.bfloat16


def colshift(v, b, width):
    if b == 1:
        return v
    lanes = v.shape[1]
    col = lax.broadcasted_iota(jnp.int32, v.shape, 1) % width
    if b == 0:
        return jnp.where(col == 0, 0.0, pltpu.roll(v, 1, 1))
    return jnp.where(col == width - 1, 0.0, pltpu.roll(v, lanes - 1, 1))


def rounded(v):
    return v.astype(BF16).astype(F32)


def dot(a, b):
    return jnp.dot(a, b, preferred_element_type=F32)


def dot_split(v, m):
    high = v.astype(BF16)
    low = (v - high.astype(F32)).astype(BF16)
    return dot(high, m) + dot(low, m)


def cdf_of(v):
    return 0.5 + 0.5 * lax.erf(v * (1.0 / math.sqrt(2.0)))


def gelu_slope(v, cdf):
    return cdf + v * (jnp.exp(-0.5 * v * v) * (1.0 / math.sqrt(2.0 * math.pi)))


def unit_of(f):
    inv = lax.rsqrt(jnp.sum(f * f, 0, keepdims=True) + 1e-06)
    return f * inv, inv


def lpips(f_dec, f_tgt, lin, count):
    unit, inv = unit_of(f_dec)
    unit_tgt, _ = unit_of(f_tgt)
    differ = unit - unit_tgt
    scaled = lin * differ * (1.0 / count)
    part = jnp.sum(scaled * differ, 0, keepdims=True)
    grad = 2.0 * scaled
    return part, (grad - unit * jnp.sum(grad * unit, 0, keepdims=True)) * inv


NAMES = (
    "img_t", "img_d", "pb", "xt", "xd", "x3t", "x3d", "x4t", "x4d", "xg4", "xg3", "xg2", "act2t",
    "act4t", "gf1", "s1", "s2", "s3", "gdec", "lacc", "slot_r", "slot_c", "w2", "w2t", "w3",
    "w3t", "w4", "w4t", "few", "vec", "tbuf", "wg",
)
MESSAGES = ("t", "d", "pt", "pd", "3t", "3d", "g4", "g3", "g2", "gd")


def message_shapes(C1, C2, W):
    Wh = W // 2
    return {
        "t": ((8, 2 * W), F32),
        "d": ((8, 3 * W), F32),
        "pt": ((C1, Wh), BF16),
        "pd": ((C1, Wh), BF16),
        "3t": ((C2, Wh), BF16),
        "3d": ((C2, Wh), BF16),
        "g4": ((C2, Wh), BF16),
        "g3": ((C2, Wh), BF16),
        "g2": ((C1, W), BF16),
        "gd": ((8, 2 * W), F32),
    }


def kernel_body(
    dims, feat, tgt, wo_raw, w1_raw, w2_raw, w3_raw, w4_raw, ob_raw, b1_raw, b2_raw, l1_raw,
    b3_raw, b4_raw, l2_raw, fg_out, red_out, *scratch
):
    R, W, C1, C2, CF, nrow, nclip = dims
    Wh, Rh = W // 2, R // 2
    H = R * nrow
    s = dict(zip(NAMES, scratch))
    rest = scratch[len(NAMES):]
    w2, w2t, w3, w3t, w4, w4t = (s[n] for n in ("w2", "w2t", "w3", "w3t", "w4", "w4t"))
    bufs = {}
    for k, name in enumerate(MESSAGES):
        bufs[name] = rest[4 * k : 4 * k + 4]
    send_sem, recv_sem, all_send, all_recv = rest[4 * len(MESSAGES):]

    me_r, me_c = lax.axis_index("row"), lax.axis_index("clip")
    keep_up = jnp.where(me_r > 0, 1.0, 0.0).astype(F32)
    keep_dn = jnp.where(me_r < nrow - 1, 1.0, 0.0).astype(F32)
    up, dn = (me_r + nrow - 1) % nrow, (me_r + 1) % nrow

    barrier = pltpu.get_barrier_semaphore()
    for k in range(1, nrow):
        pl.semaphore_signal(
            barrier, inc=1, device_id={"row": (me_r + k) % nrow}, device_id_type=pl.DeviceIdType.MESH
        )
    for k in range(1, nclip):
        pl.semaphore_signal(
            barrier, inc=1, device_id={"clip": (me_c + k) % nclip}, device_id_type=pl.DeviceIdType.MESH
        )

    def copies(name):
        k = MESSAGES.index(name)
        su, sd, ru, rd = bufs[name]
        to_up = pltpu.make_async_remote_copy(
            src_ref=su, dst_ref=rd, send_sem=send_sem.at[2 * k], recv_sem=recv_sem.at[2 * k],
            device_id={"row": up}, device_id_type=pl.DeviceIdType.MESH,
        )
        to_dn = pltpu.make_async_remote_copy(
            src_ref=sd, dst_ref=ru, send_sem=send_sem.at[2 * k + 1], recv_sem=recv_sem.at[2 * k + 1],
            device_id={"row": dn}, device_id_type=pl.DeviceIdType.MESH,
        )
        return to_up, to_dn

    def send(name, up_value, dn_value):
        su, sd, _, _ = bufs[name]
        su[...] = up_value.astype(su.dtype)
        sd[...] = dn_value.astype(sd.dtype)
        a, b = copies(name)
        a.start()
        b.start()

    def receive(name):
        a, b = copies(name)
        a.wait()
        b.wait()
        _, _, ru, rd = bufs[name]
        return ru[...].astype(F32) * keep_up, rd[...].astype(F32) * keep_dn

    def span(row, count, width=W):
        start = row * width
        if not isinstance(start, int):
            start = pl.multiple_of(start, width)
        return pl.ds(start, count * width)

    def store3(ref, row, value, width):
        C = value.shape[0]
        for b in range(3):
            ref[b * C : (b + 1) * C, span(row, value.shape[1] // width, width)] = colshift(
                value, b, width
            ).astype(BF16)

    def store24(ref, row, value):
        ref[:, span(row, value.shape[1] // W)] = jnp.concatenate(
            [colshift(value, b, W) for b in range(3)], 0
        )

    def im72(ref, row, count):
        return jnp.concatenate([ref[:, span(row + a, count)] for a in range(3)], 0).astype(BF16)

    def conv(weight, ref, row, count, width):
        total = dot(weight[0], ref[:, span(row, count, width)])
        for a in range(1, 3):
            total = total + dot(weight[a], ref[:, span(row + a, count, width)])
        return total

    vec = s["vec"]
    vec[...] = jnp.zeros_like(vec)
    for k, ref in enumerate((b1_raw, b2_raw, l1_raw, b3_raw, b4_raw, l2_raw)):
        vec[k : k + 1, : ref.shape[1]] = ref[...]
    columns = vec[...].T
    b1, b2, lin1 = (columns[:C1, k : k + 1] for k in range(3))
    b3, b4, lin2 = (columns[:C2, k : k + 1] for k in range(3, 6))
    sub = lax.broadcasted_iota(jnp.int32, (8, 1), 0)

    def column(values, fill):
        out = jnp.full((8, 1), fill, F32)
        for k in range(3):
            out = jnp.where(sub == k, values[k], out)
        return out

    obias = column([ob_raw[k] for k in range(3)], 0.0)
    shift, scale = column(shift_values, 0.0), column(scale_values, 1.0)
    lane = lambda shape, dim: lax.broadcasted_iota(jnp.int32, shape, dim)
    pool_m = jnp.where(lane((W, Wh), 0) // 2 == lane((W, Wh), 1), 0.25, 0.0).astype(BF16)
    up_m = jnp.where(lane((Wh, W), 1) // 2 == lane((Wh, W), 0), 0.25, 0.0).astype(BF16)

    few = s["few"]
    few[...] = jnp.zeros_like(few)

    def spread(k, raw, flip):
        for i in range(3):
            for a in range(3):
                rows = raw[i, 2 - a if flip else a].astype(F32)
                for b in range(3):
                    c = 2 - b if flip else b
                    at = (a * 3 + b) * 8 + i
                    few[k, at : at + 1, : rows.shape[1]] = rows[c : c + 1]

    def normal(v):
        return rounded((v - shift) / scale)

    pb = s["pb"]

    def partials(weight, source, rows):
        for i in rows:
            T = dot(weight, source(i))
            for a in range(3):
                part = colshift(T[24 * a : 24 * a + 8], 0, W)
                part = part + T[24 * a + 8 : 24 * a + 16]
                part = part + colshift(T[24 * a + 16 : 24 * a + 24], 2, W)
                at = span(i + 2 - a, 1)
                pb[:, at] = pb[:, at] + part

    spread(0, wo_raw, False)
    spread(1, w1_raw, False)
    w1 = few[1].T[:C1, :72].astype(BF16)
    tbuf = s["tbuf"]
    tbuf[...] = jnp.zeros_like(tbuf)
    for i in range(3):
        rows = tgt[i].astype(F32)
        for r in range(R):
            tbuf[i : i + 1, r * W : (r + 1) * W] = rows[r : r + 1]
    t_img = normal(tbuf[...])
    pl.semaphore_wait(barrier, nrow - 1 + nclip - 1)
    send("t", t_img[:, : 2 * W], t_img[:, (R - 2) * W :])
    store24(s["img_t"], 2, t_img)
    pb[...] = jnp.zeros_like(pb)
    partials(few[0, :72, :CF].astype(BF16), lambda i: feat[:, span(i, 1)], range(R))
    send("d", pb[:, : 3 * W], pb[:, (R - 1) * W :])

    for a in range(3):
        for b in range(3):
            w2[a, :, b * C1 : (b + 1) * C1] = w2_raw[a, b]
            w3[a, :, b * C1 : (b + 1) * C1] = w3_raw[a, b].T
            w3t[a, :, b * C2 : (b + 1) * C2] = w3_raw[2 - a, 2 - b]
            w4[a, :, b * C2 : (b + 1) * C2] = w4_raw[a, b]

    above, below = receive("t")
    store24(s["img_t"], 0, above)
    store24(s["img_t"], R + 2, below)

    def block_one(img, x, tail, save):
        def first(i, carry):
            row = 2 * i
            pre = dot(w1, im72(img, row, 2)) + b1
            cdf = cdf_of(pre)
            act = pre * cdf
            if save:
                s["s1"][:, span(row, 2)] = gelu_slope(pre, cdf)
            col = lax.broadcasted_iota(jnp.int32, (1, 2 * W), 1)
            m_first = jnp.where(i == 0, keep_up, 1.0)
            m_last = jnp.where(i == R // 2, keep_dn, 1.0)
            act = act * jnp.where(col < W, m_first, m_last)
            store3(x, row, act, W)
            return carry

        lax.fori_loop(0, R // 2 + 1, first, 0)

        def second(i, carry):
            pre = conv(w2, x, 2 * i, 2, W) + b2
            cdf = cdf_of(pre)
            act = pre * cdf
            tail(i, pre, cdf, act)
            return carry

        lax.fori_loop(0, Rh, second, 0)

    def pooled_of(act):
        return rounded(dot_split(act[:, :W] + act[:, W:], pool_m))

    def tail_target(i, pre, cdf, act):
        s["act2t"][:, span(2 * i, 2)] = act
        store3(s["x3t"], i + 1, pooled_of(act), Wh)

    def tail_decoded(i, pre, cdf, act):
        store3(s["x3d"], i + 1, pooled_of(act), Wh)
        s["s2"][:, span(2 * i, 2)] = gelu_slope(pre, cdf)
        part, grad = lpips(act, s["act2t"][:, span(2 * i, 2)], lin1, float(H * W))
        s["gf1"][:, span(2 * i, 2)] = grad
        s["lacc"][0:1, :] = s["lacc"][0:1, :] + part

    s["lacc"][...] = jnp.zeros_like(s["lacc"])
    block_one(s["img_t"], s["xt"], tail_target, False)

    def edges(ref, C, rows, width):
        return ref[C : 2 * C, width : 2 * width], ref[C : 2 * C, rows * width : (rows + 1) * width]

    def halo(name, ref, rows, width):
        above, below = receive(name)
        store3(ref, 0, above, width)
        store3(ref, rows + 1, below, width)

    send("pt", *edges(s["x3t"], C1, Rh, Wh))

    above, below = receive("d")
    zero = jnp.zeros((8, W), F32)
    sums = pb[...] + jnp.concatenate(
        [above[:, W:], jnp.zeros((8, (R - 2) * W), F32), below[:, : 2 * W]], 1
    )
    dec = jnp.concatenate([above[:, :W], sums, below[:, 2 * W :]], 1)
    d_img = normal(rounded(dec + obias))
    col = lax.broadcasted_iota(jnp.int32, (1, (R + 4) * W), 1)
    d_img = d_img * jnp.where(col < 2 * W, keep_up, jnp.where(col < (R + 2) * W, 1.0, keep_dn))
    store24(s["img_d"], 0, d_img)
    block_one(s["img_d"], s["xd"], tail_decoded, True)
    send("pd", *edges(s["x3d"], C1, Rh, Wh))

    def block_three(name, x3, x4, save):
        halo(name, x3, Rh, Wh)
        pre = conv(w3, x3, 0, Rh, Wh) + b3
        cdf = cdf_of(pre)
        if save:
            s["s3"][...] = gelu_slope(pre, cdf)
        store3(x4, 1, pre * cdf, Wh)

    block_three("pt", s["x3t"], s["x4t"], False)
    send("3t", *edges(s["x4t"], C2, Rh, Wh))
    block_three("pd", s["x3d"], s["x4d"], True)
    send("3d", *edges(s["x4d"], C2, Rh, Wh))
    for a in range(3):
        for b in range(3):
            w4t[a, :, b * C2 : (b + 1) * C2] = w4_raw[2 - a, 2 - b].T
    halo("3t", s["x4t"], Rh, Wh)
    pre = conv(w4, s["x4t"], 0, Rh, Wh) + b4
    s["act4t"][...] = pre * cdf_of(pre)
    halo("3d", s["x4d"], Rh, Wh)
    pre = conv(w4, s["x4d"], 0, Rh, Wh) + b4
    cdf = cdf_of(pre)
    part, grad = lpips(pre * cdf, s["act4t"][...], lin2, float((H // 2) * Wh))
    s["lacc"][1:2, : Rh * Wh] = part
    store3(s["xg4"], 1, grad * gelu_slope(pre, cdf), Wh)
    send("g4", *edges(s["xg4"], C2, Rh, Wh))
    for a in range(3):
        for b in range(3):
            w2t[a, :, b * C1 : (b + 1) * C1] = w2_raw[2 - a, 2 - b].T
    spread(0, wo_raw, True)
    spread(1, w1_raw, True)
    w1b = few[1, :72, :C1].astype(BF16)
    wf = few[0].T[:CF, :72].astype(BF16)

    def g3_rows(row, count):
        g3 = conv(w4t, s["xg4"], row, count, Wh) * s["s3"][:, span(row, count, Wh)]
        store3(s["xg3"], row + 1, g3, Wh)

    g3_rows(1, Rh - 2)
    halo("g4", s["xg4"], Rh, Wh)
    g3_rows(0, 1)
    g3_rows(Rh - 1, 1)
    send("g3", *edges(s["xg3"], C2, Rh, Wh))

    def g2_rows(first, count):
        gpool = conv(w3t, s["xg3"], first, count, Wh)
        for i in range(count):
            wide = dot_split(gpool[:, i * Wh : (i + 1) * Wh], up_m)
            for j in range(2):
                row = 2 * (first + i) + j
                g2 = (s["gf1"][:, span(row, 1)] + wide) * s["s2"][:, span(row, 1)]
                store3(s["xg2"], row + 1, g2, W)

    g2_rows(1, Rh - 2)
    halo("g3", s["xg3"], Rh, Wh)
    g2_rows(0, 1)
    g2_rows(Rh - 1, 1)
    send("g2", *edges(s["xg2"], C1, R, W))

    def g1_row(i):
        g1 = conv(w2t, s["xg2"], i, 1, W) * s["s1"][:, span(i + 1, 1)]
        return g1.astype(BF16)

    pb[...] = jnp.zeros_like(pb)
    partials(w1b, g1_row, range(1, R - 1))
    halo("g2", s["xg2"], R, W)
    partials(w1b, g1_row, (0, R - 1))
    send("gd", pb[:, : 2 * W], pb[:, R * W :])

    bias_grad = jnp.zeros((8, 1), F32)
    wgrad = jnp.zeros((72, CF), F32)

    def weight_terms(i):
        return lax.dot_general(
            im72(s["gdec"], i, 1), feat[:, span(i, 1)], (((1,), (1,)), ((), ())),
            preferred_element_type=F32,
        )

    middle = rounded(pb[:, span(2, R - 2)] / scale)
    store24(s["gdec"], 2, middle)
    for i in range(2, R - 2):
        wgrad = wgrad + weight_terms(i)
    above, below = receive("gd")
    first_two = rounded((pb[:, span(0, 2)] + above) / scale)
    last_two = rounded((pb[:, span(R, 2)] + below) / scale)
    col = lax.broadcasted_iota(jnp.int32, (1, 2 * W), 1)
    first_two = first_two * jnp.where(col < W, keep_up, 1.0)
    last_two = last_two * jnp.where(col < W, 1.0, keep_dn)
    store24(s["gdec"], 0, first_two)
    store24(s["gdec"], R, last_two)
    for i in (0, 1, R - 2, R - 1):
        wgrad = wgrad + weight_terms(i)
    for own in (middle, first_two[:, W:], last_two[:, :W]):
        bias_grad = bias_grad + jnp.sum(own, 1, keepdims=True)
    loss = jnp.sum(jnp.sum(s["lacc"][...], 0, keepdims=True), 1, keepdims=True)

    def everyone(axis, me, size, slots, base):
        out = []
        for k in range(1, size):
            out.append(
                pltpu.make_async_remote_copy(
                    src_ref=slots.at[me], dst_ref=slots.at[me],
                    send_sem=all_send.at[base + k], recv_sem=all_recv.at[base + k],
                    device_id={axis: (me + k) % size}, device_id_type=pl.DeviceIdType.MESH,
                )
            )
        return out

    slot_r, slot_c = s["slot_r"], s["slot_c"]
    wg = s["wg"]
    wg[:72] = wgrad
    wg[72:80] = jnp.broadcast_to(bias_grad, (8, CF))
    for o in range(3):
        for tap in range(9):
            slot_r[me_r, o * 9 + 8 - tap] = wg[tap * 8 + o]
        slot_r[me_r, 27 + o] = wg[72 + o]
    slot_r[me_r, 30:32] = jnp.broadcast_to(loss, (2, CF))
    first = everyone("row", me_r, nrow, slot_r, 0)
    for c in first:
        c.start()
    for i in range(R // 2):
        fg_out[:, span(i, 1)] = dot(wf, im72(s["gdec"], i, 1)).astype(BF16)
    for c in first:
        c.wait()
    total = slot_r[0]
    for k in range(1, nrow):
        total = total + slot_r[k]
    slot_c[me_c] = total
    second = everyone("clip", me_c, nclip, slot_c, nrow)
    for c in second:
        c.start()
    for i in range(R // 2, R):
        fg_out[:, span(i, 1)] = dot(wf, im72(s["gdec"], i, 1)).astype(BF16)
    for c in second:
        c.wait()
    total = slot_c[0]
    for k in range(1, nclip):
        total = total + slot_c[k]
    red_out[...] = total


def local(
    features, out_weight, out_bias, targets, weight_one, bias_one, weight_two, bias_two,
    weight_three, bias_three, weight_four, bias_four, lin_one, lin_two,
):
    _, CF, R, W = features.shape
    C1, C2 = weight_two.shape[0], weight_four.shape[0]
    nrow, nclip = lax.axis_size("row"), lax.axis_size("clip")
    Wh, Rh = W // 2, R // 2
    operands = (
        features.reshape(CF, R * W), targets[0], out_weight.transpose(0, 2, 3, 1),
        weight_one.transpose(1, 2, 3, 0), weight_two.transpose(2, 3, 0, 1),
        weight_three.transpose(2, 3, 1, 0), weight_four.transpose(2, 3, 0, 1), out_bias,
        bias_one[None], bias_two[None], lin_one[None], bias_three[None], bias_four[None],
        lin_two[None],
    )
    V = pltpu.VMEM
    scratch = [
        V((24, (R + 4) * W), F32), V((24, (R + 4) * W), F32), V((8, (R + 2) * W), F32),
        V((3 * C1, (R + 2) * W), BF16), V((3 * C1, (R + 2) * W), BF16),
        V((3 * C1, (Rh + 2) * Wh), BF16), V((3 * C1, (Rh + 2) * Wh), BF16),
        V((3 * C2, (Rh + 2) * Wh), BF16), V((3 * C2, (Rh + 2) * Wh), BF16),
        V((3 * C2, (Rh + 2) * Wh), BF16), V((3 * C2, (Rh + 2) * Wh), BF16),
        V((3 * C1, (R + 2) * W), BF16),
        V((C1, R * W), F32), V((C2, Rh * Wh), F32), V((C1, R * W), F32),
        V((C1, (R + 2) * W), F32), V((C1, R * W), F32), V((C2, Rh * Wh), F32),
        V((24, (R + 2) * W), F32), V((8, 2 * W), F32),
        V((nrow, 32, CF), F32), V((nclip, 32, CF), F32),
        V((3, C1, 3 * C1), BF16), V((3, C1, 3 * C1), BF16), V((3, C2, 3 * C1), BF16),
        V((3, C1, 3 * C2), BF16), V((3, C2, 3 * C2), BF16), V((3, C2, 3 * C2), BF16),
        V((2, 128, max(CF, C1, 128)), F32), V((8, 128), F32), V((8, R * W), F32), V((80, CF), F32),
    ]
    shapes = message_shapes(C1, C2, W)
    for name in MESSAGES:
        scratch += [V(*shapes[name])] * 4
    D = pltpu.SemaphoreType.DMA
    scratch += [D((2 * len(MESSAGES),)), D((2 * len(MESSAGES),)), D((nrow + nclip,)), D((nrow + nclip,))]
    vmem = pl.BlockSpec(memory_space=pltpu.VMEM)
    fg, red = pl.pallas_call(
        functools.partial(kernel_body, (R, W, C1, C2, CF, nrow, nclip)),
        out_shape=(
            jax.ShapeDtypeStruct((CF, R * W), BF16),
            jax.ShapeDtypeStruct((32, CF), F32),
        ),
        in_specs=[vmem] * 7 + [pl.BlockSpec(memory_space=pltpu.SMEM)] + [vmem] * 6,
        out_specs=(vmem, vmem),
        scratch_shapes=scratch,
        name="lpips_step",
        compiler_params=pltpu.CompilerParams(
            collective_id=0, has_side_effects=True, vmem_limit_bytes=62 * 1024 * 1024
        ),
    )(*operands)
    feature_grad = fg.reshape(1, CF, R, W)
    weight_grad = red[:27].reshape(3, 3, 3, CF).transpose(0, 3, 1, 2)
    return (red[30, 0], feature_grad, weight_grad, red[27:30, 0])


def solution(mesh):
    placed = [P()] * 14
    placed[0] = placed[3] = P("clip", None, "row", None)
    return jax.shard_map(
        local,
        mesh=mesh,
        in_specs=tuple(placed),
        out_specs=(P(), P("clip", None, "row", None), P(), P()),
        check_vma=False,
    )
```
